512 devices in a mesh: hid: 32 (over z, core), out: 8 (over y, x_lo), rep: 2 (over x_hi).
Axes of the slice: x: 4 (x_hi: 2, x_lo: 2; x = x_hi * 2 + x_lo), y: 4, z: 16, core: 2. Of those that a mesh axis runs over, the one named last changes fastest.
Arguments:
- x_act: bfloat16 [2, 512, 28672], P('rep', None, 'hid'), may hold values from -6 to 6
- out_grad: bfloat16 [2, 512, 4096], P('rep', None, 'out'), may hold values from -6 to 6
- weight_codes: int32 [4096, 28672], P(('out', 'rep'), 'hid'), may hold values from -127 to 127
- group_exps: int32 [4096, 224], P(('out', 'rep'), 'hid'), may hold values from -13 to -11
- local_factor: bfloat16 [896, 896], P(('out', 'rep')), may hold values from -0.1875 to 0.1875
- first_moment: bfloat16 [4096, 28672], P(('out', 'rep'), 'hid'), may hold values from -6 to 6
- second_moment: bfloat16 [4096, 28672], P(('out', 'rep'), 'hid'), may hold values from 1 to 8
Outputs:
- input_grad: bfloat16 [2, 512, 28672], P('rep', 'out', 'hid')
- weight_step: bfloat16 [4096, 28672], P(('out', 'rep'), 'hid')
- new_first: bfloat16 [4096, 28672], P(('out', 'rep'), 'hid')
- new_second: bfloat16 [4096, 28672], P(('out', 'rep'), 'hid')
The draws below stay inside these ranges and needn't reach their ends.
All inputs are finite; a program needn't handle non-finite values.
Results may differ from the reference program's by a relative error of at most 0.0049.
Values may be sent and summed in bfloat16 or wider, within the bound.
No kernel may reach another device: no remote copies, remote signals or barrier semaphores. Data moves between devices by JAX's collectives and lax.ppermute only.
A program may use at most 64 MiB of HBM per device.

```python
import math
import jax
import jax.numpy as jnp
from jax import lax

LOCAL = 896
GROUP = 128
ROWS_DEV = 512
FF = 28672
DW = 4096
N_HID = 32
N_REP = 2


def place_ends(result, own_key, smallest, top_value):
    longest = result.shape.index(max(result.shape))
    spots = []
    for shift in (0, 1):
        where = [jax.random.randint(jax.random.fold_in(own_key, axis), (), 0, length) for axis, length in enumerate(result.shape)]
        where[longest] = (where[longest] + shift) % result.shape[longest]
        spots.append(tuple(where))
    return result.at[spots[0]].set(smallest).at[spots[1]].set(top_value)


def block_levels(rng, extent, shards, low, high):
    gain = 1.0
    for position, shards_of in shards:
        draws = jax.random.uniform(jax.random.fold_in(jax.random.fold_in(rng, 6), position), (shards_of,), jnp.float32, low / len(shards), high / len(shards))
        gain = gain * jnp.repeat(jnp.exp(draws), extent[position] // shards_of).reshape((-1,) + (1,) * (len(extent) - 1 - position))
    return gain


def gaussian(stream_key, extent, width, limit, split=(), kind=jnp.bfloat16):
    array = width * jax.random.normal(stream_key, extent, jnp.float32)
    if split:
        array = array * block_levels(stream_key, extent, split, -0.22, 0.18)
    return jnp.clip(array, -limit, limit).astype(kind)


def setup_inputs(seed: int = 0) -> dict:
    splits = jax.random.split(jax.random.key(seed), 8)
    x_act = gaussian(splits[0], (N_REP, ROWS_DEV, FF), 1.0, 6.0, ((0, 2), (2, 32)))
    out_grad = gaussian(splits[1], (N_REP, ROWS_DEV, DW), 1.0, 6.0, ((0, 2), (2, 8)))
    weight_codes = place_ends(jax.random.randint(splits[2], (DW, FF), -127, 128), jax.random.fold_in(splits[2], 1), -127, 127).astype(jnp.int32)
    group_exps = place_ends(jax.random.randint(splits[3], (DW, FF // GROUP), -13, -10), jax.random.fold_in(splits[3], 1), -13, (-10) - 1).astype(jnp.int32)
    local_factor = gaussian(splits[4], (LOCAL, LOCAL), LOCAL ** -0.5, 0.1875, ((0, 16),))
    first_moment = gaussian(splits[5], (DW, FF), 1.0, 6.0, ((0, 16), (1, 32)))
    second_moment = jnp.clip(jnp.exp(math.log(8.0) - 2.0794415 * jax.random.uniform(splits[6], (DW, FF), jnp.float32) ** block_levels(splits[6], (DW, FF), ((0, 16), (1, 32)), -0.2, 0.2)), 1.0, 8.0).astype(jnp.bfloat16)
    return {"x_act": x_act, "out_grad": out_grad, "weight_codes": weight_codes, "group_exps": group_exps, "local_factor": local_factor, "first_moment": first_moment, "second_moment": second_moment}


def sylvester(count):
    index_row = jnp.arange(count, dtype=jnp.int32)
    anded = jnp.bitwise_and(index_row[:, None], index_row[None, :])
    parity = jnp.zeros((count, count), jnp.int32)
    for bit_index in range(16):
        parity = parity + jnp.bitwise_and(jnp.right_shift(anded, bit_index), 1)
    return (1 - 2 * (parity % 2)).astype(jnp.float32)

def mix_blocks(values):
    signs = sylvester(N_HID)
    mixed = jnp.einsum('ral,ab->rbl', values, signs, precision=lax.Precision.HIGHEST)
    return mixed / jnp.sqrt(jnp.float32(N_HID))

def reference(x_act, out_grad, weight_codes, group_exps, local_factor, first_moment, second_moment):
    row_count = N_REP * ROWS_DEV
    factor = local_factor.astype(jnp.float32)
    x_blocks = x_act.reshape(row_count, N_HID, LOCAL).astype(jnp.float32)
    pre_mix = jnp.einsum('ral,lk->rak', x_blocks, factor)
    x_rot = mix_blocks(pre_mix).astype(jnp.bfloat16).reshape(row_count, FF)
    scales = jnp.exp2(group_exps.astype(jnp.float32))
    w_deq = weight_codes.astype(jnp.float32).reshape(DW, FF // GROUP, GROUP) * scales[:, :, None]
    w_deq = w_deq.reshape(DW, FF).astype(jnp.bfloat16)
    grads_out = out_grad.reshape(row_count, DW)
    grad_rot = jnp.dot(grads_out, w_deq, preferred_element_type=jnp.float32).astype(jnp.bfloat16)
    grad_blocks = grad_rot.reshape(row_count, N_HID, LOCAL).astype(jnp.float32)
    back_pre = jnp.einsum('ral,kl->rak', grad_blocks, factor)
    input_grad = mix_blocks(back_pre).astype(jnp.bfloat16).reshape(N_REP, ROWS_DEV, FF)
    weight_grad = jnp.dot(grads_out.T, x_rot, preferred_element_type=jnp.float32)
    gradient = jnp.where(jnp.abs(weight_codes) <= 126, weight_grad / 16.0, jnp.float32(0.0))
    moment_one = 0.9 * first_moment.astype(jnp.float32) + 0.1 * gradient
    moment_two = 0.95 * second_moment.astype(jnp.float32) + 0.05 * gradient * gradient
    corr_one = 1.0 - 0.9 ** 20
    corr_two = 1.0 - 0.95 ** 20
    weight_step = moment_one / corr_one / (jnp.sqrt(moment_two / corr_two) + 1e-08)
    return (input_grad, weight_step.astype(jnp.bfloat16), moment_one.astype(jnp.bfloat16), moment_two.astype(jnp.bfloat16))
```

```python
import math

import jax
import jax.numpy as jnp
from jax import lax
from jax.sharding import PartitionSpec as P

GROUP = 128


def trade(block, axis):
    return lax.all_to_all(block, axis, split_axis=0, concat_axis=0, tiled=True)


def spread(block, axis, count):
    return trade(jnp.broadcast_to(block[None], (count,) + block.shape), axis)


def sign_rows(count, inner):
    index = jnp.arange(count * inner, dtype=jnp.int32)
    upper, lower = index // inner, index % inner
    both = upper[:, None] & upper[None, :]
    parity = lax.population_count(both) % 2
    same = (lower[:, None] == lower[None, :]).astype(jnp.int32)
    return ((1 - 2 * parity) * same).astype(jnp.float32)


def mix_local(rows, signs, count):
    mixed = jnp.dot(signs, rows, precision=lax.Precision.HIGHEST)
    return (mixed / math.sqrt(count)).astype(jnp.bfloat16)


def swap(block):
    return lax.ppermute(block, "rep", [(0, 1), (1, 0)])


def shards(x_act, out_grad, weight_codes, group_exps, local_factor, first_moment, second_moment):
    hid_count, out_count = lax.axis_size("hid"), lax.axis_size("out")
    rep_count = lax.axis_size("rep")
    out_index, rep_index = lax.axis_index("out"), lax.axis_index("rep")
    token_count, width = x_act.shape[1:]
    mine = token_count // out_count
    few = mine // hid_count
    code_rows = weight_codes.shape[0]
    grads_out = out_grad[0]
    signs = sign_rows(hid_count, few)

    scales = jnp.exp2(group_exps.astype(jnp.float32))
    w_deq = (
        weight_codes.astype(jnp.float32).reshape(code_rows, width // GROUP, GROUP)
        * scales[:, :, None]
    )
    w_deq = w_deq.reshape(code_rows, width).astype(jnp.bfloat16)
    w_other = swap(w_deq)
    factor = spread(local_factor, ("out", "rep"), out_count * rep_count).reshape(width, width)

    tokens = lax.dynamic_slice_in_dim(x_act[0], out_index * mine, mine, axis=0)
    rows = trade(tokens.reshape(hid_count, few, width), "hid").reshape(mine, width)

    g_own = lax.dynamic_slice_in_dim(grads_out, rep_index * code_rows, code_rows, axis=1)
    g_other = lax.dynamic_slice_in_dim(grads_out, (1 - rep_index) * code_rows, code_rows, axis=1)
    partial_rot = jnp.dot(g_own, w_deq, preferred_element_type=jnp.float32) + jnp.dot(
        g_other, w_other, preferred_element_type=jnp.float32
    )
    pieces = trade(partial_rot.astype(jnp.bfloat16).reshape(out_count, mine, width), "out")

    pre_mix = jnp.dot(rows, factor, preferred_element_type=jnp.float32)
    rotated = mix_local(pre_mix, signs, hid_count)
    x_part = trade(rotated.reshape(hid_count, few, width), "hid").reshape(mine, width)

    grad_rot = pieces.astype(jnp.float32).sum(axis=0).astype(jnp.bfloat16)
    grad_rows = trade(grad_rot.reshape(hid_count, few, width), "hid").reshape(mine, width)
    x_rot = spread(x_part, "out", out_count).reshape(token_count, width)

    back_pre = lax.dot_general(
        grad_rows, factor, (((1,), (1,)), ((), ())), preferred_element_type=jnp.float32
    )
    back = mix_local(back_pre, signs, hid_count)
    input_grad = trade(back.reshape(hid_count, few, width), "hid").reshape(1, mine, width)

    contract = (((0,), (0,)), ((), ()))
    away = lax.dot_general(g_other, x_rot, contract, preferred_element_type=jnp.float32)
    arrived = swap(away.astype(jnp.bfloat16))
    weight_grad = lax.dot_general(
        g_own, x_rot, contract, preferred_element_type=jnp.float32
    ) + arrived.astype(jnp.float32)

    gradient = jnp.where(jnp.abs(weight_codes) <= 126, weight_grad / 16.0, jnp.float32(0.0))
    moment_one = 0.9 * first_moment.astype(jnp.float32) + 0.1 * gradient
    moment_two = 0.95 * second_moment.astype(jnp.float32) + 0.05 * gradient * gradient
    corr_one = 1.0 - 0.9**20
    corr_two = 1.0 - 0.95**20
    weight_step = moment_one / corr_one / (jnp.sqrt(moment_two / corr_two) + 1e-08)
    return (
        input_grad,
        weight_step.astype(jnp.bfloat16),
        moment_one.astype(jnp.bfloat16),
        moment_two.astype(jnp.bfloat16),
    )


def solution(mesh):
    placed = (
        P("rep", None, "hid"),
        P("rep", None, "out"),
        P(("out", "rep"), "hid"),
        P(("out", "rep"), "hid"),
        P(("out", "rep"), None),
        P(("out", "rep"), "hid"),
        P(("out", "rep"), "hid"),
    )
    return jax.shard_map(
        shards,
        mesh=mesh,
        in_specs=placed,
        out_specs=(
            P("rep", "out", "hid"),
            P(("out", "rep"), "hid"),
            P(("out", "rep"), "hid"),
            P(("out", "rep"), "hid"),
        ),
        check_vma=False,
    )
```

```python
import math

import jax
import jax.numpy as jnp
import numpy as np
from jax import lax
from jax.sharding import PartitionSpec as P

GROUP = 128


def trade(block, axis):
    return lax.all_to_all(block, axis, split_axis=0, concat_axis=0, tiled=True)


def spread(block, axis, count):
    return trade(jnp.broadcast_to(block[None], (count,) + block.shape), axis)


def partner(block, axis, bit):
    count = lax.axis_size(axis)
    return lax.ppermute(block, axis, [(s, s ^ bit) for s in range(count)])


def join(mine, other, upper, axis=0):
    return jnp.where(
        upper, jnp.stack([other, mine], axis=axis), jnp.stack([mine, other], axis=axis)
    )


def sign_rows(count, inner):
    index = np.arange(count * inner)
    upper, lower = index // inner, index % inner
    both = upper[:, None] & upper[None, :]
    parity = np.zeros_like(both)
    for bit in range(count.bit_length()):
        parity ^= both >> bit & 1
    same = lower[:, None] == lower[None, :]
    return ((1 - 2 * parity) * same).astype(np.float32)


def gather_factor(local_factor):
    core = lax.axis_index("hid") % 2
    rows, width = local_factor.shape
    other = partner(local_factor, "rep", 1)
    block = jnp.where(core == lax.axis_index("rep"), local_factor, other)[None]
    for bit in range(lax.axis_size("out").bit_length() - 1):
        upper = (lax.axis_index("out") >> bit & 1) == 1
        block = join(block, partner(block, "out", 1 << bit), upper).reshape(-1, rows, width)
    return join(block, partner(block, "hid", 1), core == 1, axis=1).reshape(width, width)


def shards(x_act, out_grad, weight_codes, group_exps, local_factor, first_moment, second_moment):
    hid_count, out_count = lax.axis_size("hid"), lax.axis_size("out")
    out_index, rep_index = lax.axis_index("out"), lax.axis_index("rep")
    token_count, width = x_act.shape[1:]
    mine = token_count // out_count
    few = mine // hid_count
    code_rows = weight_codes.shape[0]
    grads_out = out_grad[0]
    signs = sign_rows(hid_count, few)
    root = math.sqrt(hid_count)

    tokens = lax.dynamic_slice_in_dim(x_act[0], out_index * mine, mine, axis=0)
    rows = trade(tokens.reshape(hid_count, few, width), "hid").reshape(mine, width)

    scales = jnp.exp2(group_exps.astype(jnp.float32)).astype(jnp.bfloat16)
    lanes = np.repeat(np.eye(width // GROUP, dtype=np.float32), GROUP, axis=1)
    scales = jnp.dot(scales, lanes.astype(jnp.bfloat16), preferred_element_type=jnp.float32)
    w_deq = (weight_codes.astype(jnp.float32) * scales).astype(jnp.bfloat16)
    w_other = partner(w_deq, "rep", 1)
    factor = gather_factor(local_factor)

    g_own = lax.dynamic_slice_in_dim(grads_out, rep_index * code_rows, code_rows, axis=1)
    g_other = lax.dynamic_slice_in_dim(grads_out, (1 - rep_index) * code_rows, code_rows, axis=1)
    partial_rot = jnp.dot(g_own, w_deq, preferred_element_type=jnp.float32) + jnp.dot(
        g_other, w_other, preferred_element_type=jnp.float32
    )
    pieces = trade(partial_rot.astype(jnp.bfloat16).reshape(out_count, mine, width), "out")

    mixed = jnp.dot(signs.astype(jnp.bfloat16), rows, preferred_element_type=jnp.float32) / root
    mixed = mixed.astype(jnp.bfloat16)
    grad_rot = pieces.astype(jnp.float32).sum(axis=0).astype(jnp.bfloat16)
    sent = jnp.concatenate(
        [mixed.reshape(hid_count, few, width), grad_rot.reshape(hid_count, few, width)], axis=1
    )
    got = trade(sent, "hid")
    mixed, grad_rows = got[:, :few].reshape(mine, width), got[:, few:].reshape(mine, width)

    x_part = jnp.dot(mixed, factor, preferred_element_type=jnp.float32).astype(jnp.bfloat16)
    x_rot = spread(x_part, "out", out_count).reshape(token_count, width)

    back = lax.dot_general(
        grad_rows, factor, (((1,), (1,)), ((), ())), preferred_element_type=jnp.float32
    )
    back = jnp.dot(signs, back, precision=lax.Precision.HIGHEST) / root
    back = back.astype(jnp.bfloat16).reshape(hid_count, few, width)
    input_grad = trade(back, "hid").reshape(1, mine, width)

    contract = (((0,), (0,)), ((), ()))
    away = lax.dot_general(g_other, x_rot, contract, preferred_element_type=jnp.float32)
    arrived = partner(away.astype(jnp.bfloat16), "rep", 1)
    weight_grad = lax.dot_general(
        g_own, x_rot, contract, preferred_element_type=jnp.float32
    ) + arrived.astype(jnp.float32)

    gradient = jnp.where(jnp.abs(weight_codes) <= 126, weight_grad / 16.0, jnp.float32(0.0))
    moment_one = 0.9 * first_moment.astype(jnp.float32) + 0.1 * gradient
    moment_two = 0.95 * second_moment.astype(jnp.float32) + 0.05 * gradient * gradient
    corr_one = 1.0 - 0.9**20
    corr_two = 1.0 - 0.95**20
    weight_step = moment_one / corr_one / (jnp.sqrt(moment_two / corr_two) + 1e-08)
    return (
        input_grad,
        weight_step.astype(jnp.bfloat16),
        moment_one.astype(jnp.bfloat16),
        moment_two.astype(jnp.bfloat16),
    )


def solution(mesh):
    placed = (
        P("rep", None, "hid"),
        P("rep", None, "out"),
        P(("out", "rep"), "hid"),
        P(("out", "rep"), "hid"),
        P(("out", "rep"), None),
        P(("out", "rep"), "hid"),
        P(("out", "rep"), "hid"),
    )
    return jax.shard_map(
        shards,
        mesh=mesh,
        in_specs=placed,
        out_specs=(
            P("rep", "out", "hid"),
            P(("out", "rep"), "hid"),
            P(("out", "rep"), "hid"),
            P(("out", "rep"), "hid"),
        ),
        check_vma=False,
    )
```

```python
import math

import jax
import jax.numpy as jnp
import numpy as np
from jax import lax
from jax.sharding import PartitionSpec as P


GROUP = 128


def trade(block, axis):
    return lax.all_to_all(block, axis, split_axis=0, concat_axis=0, tiled=True)


def partner(block, axis, bit):
    count = lax.axis_size(axis)
    return lax.ppermute(block, axis, [(s, s ^ bit) for s in range(count)])


def join(mine, other, upper, axis=0):
    return jnp.where(
        upper, jnp.stack([other, mine], axis=axis), jnp.stack([mine, other], axis=axis)
    )


def sign_rows(count, inner):
    index = np.arange(count * inner)
    upper, lower = index // inner, index % inner
    both = upper[:, None] & upper[None, :]
    parity = np.zeros_like(both)
    for bit in range(count.bit_length()):
        parity ^= both >> bit & 1
    same = lower[:, None] == lower[None, :]
    return ((1 - 2 * parity) * same).astype(np.float32)


def gather_factor(local_factor):
    core = lax.axis_index("hid") % 2
    rows, width = local_factor.shape
    other = partner(local_factor, "rep", 1)
    block = jnp.where(core == lax.axis_index("rep"), local_factor, other)[None]
    for bit in range(lax.axis_size("out").bit_length() - 1):
        upper = (lax.axis_index("out") >> bit & 1) == 1
        other = partner(block, "out", 1 << bit)
        block = join(block, other, upper).reshape(-1, rows, width)
    return join(block, partner(block, "hid", 1), core == 1, axis=1).reshape(width, width)


def step(x_act, out_grad, weight_codes, group_exps, local_factor, first_moment, second_moment):
    hid_count, out_count = lax.axis_size("hid"), lax.axis_size("out")
    out_index, rep_index = lax.axis_index("out"), lax.axis_index("rep")
    token_count, width = x_act.shape[1:]
    mine = token_count // out_count
    few = mine // hid_count
    code_rows = weight_codes.shape[0]
    grads_out = out_grad[0]
    signs = sign_rows(hid_count, few)
    root = math.sqrt(hid_count)

    tokens = lax.dynamic_slice_in_dim(x_act[0], out_index * mine, mine, axis=0)
    rows = trade(tokens.reshape(hid_count, few, width), "hid").reshape(mine, width)

    scales = jnp.exp2(group_exps.astype(jnp.float32)).astype(jnp.bfloat16)
    lanes = np.repeat(np.eye(width // GROUP, dtype=np.float32), GROUP, axis=1)
    scales = jnp.dot(scales, lanes.astype(jnp.bfloat16), preferred_element_type=jnp.float32)
    w_deq = (weight_codes.astype(jnp.float32) * scales).astype(jnp.bfloat16)
    w_other = partner(w_deq, "rep", 1)
    factor = gather_factor(local_factor)

    grads_t = grads_out.T
    g_own = lax.dynamic_slice_in_dim(grads_out, rep_index * code_rows, code_rows, axis=1)
    g_other = lax.dynamic_slice_in_dim(grads_out, (1 - rep_index) * code_rows, code_rows, axis=1)
    gt_own = lax.dynamic_slice_in_dim(grads_t, rep_index * code_rows, code_rows, axis=0)
    gt_other = lax.dynamic_slice_in_dim(grads_t, (1 - rep_index) * code_rows, code_rows, axis=0)
    g_own, g_other, gt_own, gt_other = lax.optimization_barrier((g_own, g_other, gt_own, gt_other))
    partial_rot = jnp.dot(g_own, w_deq, preferred_element_type=jnp.float32) + jnp.dot(
        g_other, w_other, preferred_element_type=jnp.float32
    )
    partial_rot = partial_rot.astype(jnp.bfloat16).reshape(out_count, mine, width)
    pieces = trade(partial_rot, "out")

    mixed = jnp.dot(signs.astype(jnp.bfloat16), rows, preferred_element_type=jnp.float32) / root
    mixed = mixed.astype(jnp.bfloat16)
    grad_rot = pieces.astype(jnp.float32).sum(axis=0).astype(jnp.bfloat16)
    sent = jnp.concatenate(
        [mixed.reshape(hid_count, few, width), grad_rot.reshape(hid_count, few, width)], axis=1
    )
    got = trade(sent, "hid")
    mixed, grad_rows = got[:, :few].reshape(mine, width), got[:, few:].reshape(mine, width)
    mixed = jnp.broadcast_to(mixed[None], (out_count, mine, width))
    mixed = trade(mixed, "out").reshape(token_count, width)

    back = lax.dot_general(
        grad_rows, factor, (((1,), (1,)), ((), ())), preferred_element_type=jnp.float32
    )
    back = jnp.dot(signs, back, precision=lax.Precision.HIGHEST) / root
    back = back.astype(jnp.bfloat16).reshape(hid_count, few, width)
    input_grad = trade(back, "hid").reshape(1, mine, width)

    away = jnp.dot(gt_other, mixed, preferred_element_type=jnp.float32)
    away = away.astype(jnp.bfloat16)
    arrived = partner(away, "rep", 1)
    own = jnp.dot(gt_own, mixed, preferred_element_type=jnp.float32)
    own = lax.optimization_barrier(own)
    weight_grad = (own + arrived.astype(jnp.float32)).astype(jnp.bfloat16)
    weight_grad = jnp.dot(weight_grad, factor, preferred_element_type=jnp.float32)
    return (input_grad,) + adam(weight_grad, weight_codes, first_moment, second_moment)


def adam(weight_grad, weight_codes, first_moment, second_moment):
    gradient = jnp.where(jnp.abs(weight_codes) <= 126, weight_grad / 16.0, jnp.float32(0.0))
    moment_one = 0.9 * first_moment.astype(jnp.float32) + 0.1 * gradient
    moment_two = 0.95 * second_moment.astype(jnp.float32) + 0.05 * gradient * gradient
    corr_one = 1.0 - 0.9**20
    corr_two = 1.0 - 0.95**20
    weight_step = moment_one / corr_one / (jnp.sqrt(moment_two / corr_two) + 1e-08)
    return (
        weight_step.astype(jnp.bfloat16),
        moment_one.astype(jnp.bfloat16),
        moment_two.astype(jnp.bfloat16),
    )


def solution(mesh):
    placed = (
        P("rep", None, "hid"),
        P("rep", None, "out"),
        P(("out", "rep"), "hid"),
        P(("out", "rep"), "hid"),
        P(("out", "rep"), None),
        P(("out", "rep"), "hid"),
        P(("out", "rep"), "hid"),
    )
    return jax.shard_map(
        step,
        mesh=mesh,
        in_specs=placed,
        out_specs=(
            P("rep", "out", "hid"),
            P(("out", "rep"), "hid"),
            P(("out", "rep"), "hid"),
            P(("out", "rep"), "hid"),
        ),
        check_vma=False,
    )
```

```python
import math

import jax
import jax.numpy as jnp
import numpy as np
from jax import lax
from jax.experimental import pallas as pl
from jax.experimental.pallas import tpu as pltpu
from jax.sharding import PartitionSpec as P


GROUP = 128


def trade(block, axis):
    return lax.all_to_all(block, axis, split_axis=0, concat_axis=0, tiled=True)


def partner(block, axis, bit):
    count = lax.axis_size(axis)
    return lax.ppermute(block, axis, [(s, s ^ bit) for s in range(count)])


def order_kernel(place, mine, other, out):
    spot, core = place[0], place[1]
    for index in range(mine.shape[0]):
        source = index ^ spot

        @pl.when(core == 0)
        def _():
            out[index, 0] = mine[source]
            out[index, 1] = other[source]

        @pl.when(core == 1)
        def _():
            out[index, 0] = other[source]
            out[index, 1] = mine[source]


def in_order(mine, other, spot, core):
    count, rows, width = mine.shape
    whole = pl.BlockSpec(memory_space=pltpu.VMEM)
    return pl.pallas_call(
        order_kernel,
        out_shape=jax.ShapeDtypeStruct((count, 2, rows, width), mine.dtype),
        in_specs=[pl.BlockSpec(memory_space=pltpu.SMEM), whole, whole],
        out_specs=whole,
        cost_estimate=pl.CostEstimate(
            flops=0, bytes_accessed=8 * count * rows * width, transcendentals=0
        ),
    )(jnp.stack([spot, core]), mine, other)


def sign_rows(count, inner):
    index = np.arange(count * inner)
    upper, lower = index // inner, index % inner
    both = upper[:, None] & upper[None, :]
    parity = np.zeros_like(both)
    for bit in range(count.bit_length()):
        parity ^= both >> bit & 1
    same = lower[:, None] == lower[None, :]
    return ((1 - 2 * parity) * same).astype(np.float32)


def gather_factor(local_factor):
    core, spot = lax.axis_index("hid") % 2, lax.axis_index("out")
    _, width = local_factor.shape
    bits = lax.axis_size("out").bit_length() - 1
    other = partner(local_factor, "rep", 1)
    block = jnp.where(core == lax.axis_index("rep"), local_factor, other)[None]
    for bit in range(bits):
        other = partner(block, "out", 1 << bit)
        block = jnp.concatenate([block, other], axis=0)
    other = partner(block, "hid", 1)
    return in_order(block, other, spot, core).reshape(width, width)


def mix_blocks(block):
    where = lax.axis_index("hid")
    count = lax.axis_size("hid")
    total = block
    for bit in reversed(range(count.bit_length() - 1)):
        sent = total if bit < 3 else total.astype(jnp.bfloat16)
        other = partner(sent, "hid", 1 << bit).astype(jnp.float32)
        sign = 1.0 - 2.0 * (where >> bit & 1).astype(jnp.float32)
        total = other + sign * total.astype(jnp.float32)
    return (total / math.sqrt(count)).astype(jnp.bfloat16)


def step(x_act, out_grad, weight_codes, group_exps, local_factor, first_moment, second_moment):
    hid_count, out_count = lax.axis_size("hid"), lax.axis_size("out")
    out_index, rep_index = lax.axis_index("out"), lax.axis_index("rep")
    token_count, width = x_act.shape[1:]
    mine = token_count // out_count
    few = mine // hid_count
    code_rows = weight_codes.shape[0]
    grads_out = out_grad[0]
    signs = sign_rows(hid_count, few)
    root = math.sqrt(hid_count)

    tokens = lax.dynamic_slice_in_dim(x_act[0], out_index * mine, mine, axis=0)
    mixed = mix_blocks(tokens)

    scales = jnp.exp2(group_exps.astype(jnp.float32)).astype(jnp.bfloat16)
    lanes = np.repeat(np.eye(width // GROUP, dtype=np.float32), GROUP, axis=1)
    scales = jnp.dot(scales, lanes.astype(jnp.bfloat16), preferred_element_type=jnp.float32)
    w_deq = (weight_codes.astype(jnp.float32) * scales).astype(jnp.bfloat16)
    w_other = partner(w_deq, "rep", 1)
    factor = gather_factor(local_factor)

    grads_t = grads_out.T
    g_own = lax.dynamic_slice_in_dim(grads_out, rep_index * code_rows, code_rows, axis=1)
    g_other = lax.dynamic_slice_in_dim(grads_out, (1 - rep_index) * code_rows, code_rows, axis=1)
    gt_own = lax.dynamic_slice_in_dim(grads_t, rep_index * code_rows, code_rows, axis=0)
    gt_other = lax.dynamic_slice_in_dim(grads_t, (1 - rep_index) * code_rows, code_rows, axis=0)
    g_own, g_other, gt_own, gt_other = lax.optimization_barrier((g_own, g_other, gt_own, gt_other))
    partial_rot = jnp.dot(g_own, w_deq, preferred_element_type=jnp.float32) + jnp.dot(
        g_other, w_other, preferred_element_type=jnp.float32
    )
    partial_rot = partial_rot.astype(jnp.bfloat16).reshape(out_count, mine, width)
    pieces = trade(partial_rot, "out")

    grad_rot = pieces.astype(jnp.float32).sum(axis=0).astype(jnp.bfloat16)
    grad_rows = trade(grad_rot.reshape(hid_count, few, width), "hid")
    grad_rows = grad_rows.reshape(mine, width)
    mixed = jnp.broadcast_to(mixed[None], (out_count, mine, width))
    mixed = trade(mixed, "out").reshape(token_count, width)

    back = lax.dot_general(
        grad_rows, factor, (((1,), (1,)), ((), ())), preferred_element_type=jnp.float32
    )
    back = jnp.dot(signs, back, precision=lax.Precision.HIGHEST) / root
    back = back.astype(jnp.bfloat16).reshape(hid_count, few, width)
    input_grad = trade(back, "hid").reshape(1, mine, width)

    away = jnp.dot(gt_other, mixed, preferred_element_type=jnp.float32)
    away = away.astype(jnp.bfloat16)
    arrived = partner(away, "rep", 1)
    own = jnp.dot(gt_own, mixed, preferred_element_type=jnp.float32)
    own = lax.optimization_barrier(own)
    weight_grad = (own + arrived.astype(jnp.float32)).astype(jnp.bfloat16)
    weight_grad = jnp.dot(weight_grad, factor, preferred_element_type=jnp.float32)
    return (input_grad,) + adam(weight_grad, weight_codes, first_moment, second_moment)


def adam(weight_grad, weight_codes, first_moment, second_moment):
    gradient = jnp.where(jnp.abs(weight_codes) <= 126, weight_grad / 16.0, jnp.float32(0.0))
    moment_one = 0.9 * first_moment.astype(jnp.float32) + 0.1 * gradient
    moment_two = 0.95 * second_moment.astype(jnp.float32) + 0.05 * gradient * gradient
    corr_one = 1.0 - 0.9**20
    corr_two = 1.0 - 0.95**20
    weight_step = moment_one / corr_one / (jnp.sqrt(moment_two / corr_two) + 1e-08)
    return (
        weight_step.astype(jnp.bfloat16),
        moment_one.astype(jnp.bfloat16),
        moment_two.astype(jnp.bfloat16),
    )


def solution(mesh):
    placed = (
        P("rep", None, "hid"),
        P("rep", None, "out"),
        P(("out", "rep"), "hid"),
        P(("out", "rep"), "hid"),
        P(("out", "rep"), None),
        P(("out", "rep"), "hid"),
        P(("out", "rep"), "hid"),
    )
    return jax.shard_map(
        step,
        mesh=mesh,
        in_specs=placed,
        out_specs=(
            P("rep", "out", "hid"),
            P(("out", "rep"), "hid"),
            P(("out", "rep"), "hid"),
            P(("out", "rep"), "hid"),
        ),
        check_vma=False,
    )
```

```python
import math

import jax
import jax.numpy as jnp
import numpy as np
from jax import lax
from jax.experimental import pallas as pl
from jax.experimental.pallas import tpu as pltpu
from jax.sharding import PartitionSpec as P


GROUP = 128


def trade(block, axis):
    return lax.all_to_all(block, axis, split_axis=0, concat_axis=0, tiled=True)


def partner(block, axis, bit):
    count = lax.axis_size(axis)
    return lax.ppermute(block, axis, [(s, s ^ bit) for s in range(count)])


def order_kernel(place, mine, other, out):
    spot, core = place[0], place[1]
    for index in range(mine.shape[0]):
        source = index ^ spot

        @pl.when(core == 0)
        def _():
            out[index, 0] = mine[source]
            out[index, 1] = other[source]

        @pl.when(core == 1)
        def _():
            out[index, 0] = other[source]
            out[index, 1] = mine[source]


def in_order(mine, other, spot, core):
    count, rows, width = mine.shape
    whole = pl.BlockSpec(memory_space=pltpu.VMEM)
    return pl.pallas_call(
        order_kernel,
        out_shape=jax.ShapeDtypeStruct((count, 2, rows, width), mine.dtype),
        in_specs=[pl.BlockSpec(memory_space=pltpu.SMEM), whole, whole],
        out_specs=whole,
        cost_estimate=pl.CostEstimate(
            flops=0, bytes_accessed=8 * count * rows * width, transcendentals=0
        ),
    )(jnp.stack([spot, core]), mine, other)


def sign_rows(count, inner):
    index = np.arange(count * inner)
    upper, lower = index // inner, index % inner
    both = upper[:, None] & upper[None, :]
    parity = np.zeros_like(both)
    for bit in range(count.bit_length()):
        parity ^= both >> bit & 1
    same = lower[:, None] == lower[None, :]
    return ((1 - 2 * parity) * same).astype(np.float32)


def gather_factor(local_factor):
    core, spot = lax.axis_index("hid") % 2, lax.axis_index("out")
    _, width = local_factor.shape
    bits = lax.axis_size("out").bit_length() - 1
    other = partner(local_factor, "rep", 1)
    block = jnp.where(core == lax.axis_index("rep"), local_factor, other)[None]
    for bit in range(bits):
        other = partner(block, "out", 1 << bit)
        block = jnp.concatenate([block, other], axis=0)
    other = partner(block, "hid", 1)
    return in_order(block, other, spot, core).reshape(width, width)


def mix_blocks(block):
    where = lax.axis_index("hid")
    count = lax.axis_size("hid")
    total = block
    for bit in reversed(range(count.bit_length() - 1)):
        sent = total if bit < 2 else total.astype(jnp.bfloat16)
        other = partner(sent, "hid", 1 << bit).astype(jnp.float32)
        sign = 1.0 - 2.0 * (where >> bit & 1).astype(jnp.float32)
        total = other + sign * total.astype(jnp.float32)
    return total / math.sqrt(count)


def step(x_act, out_grad, weight_codes, group_exps, local_factor, first_moment, second_moment):
    hid_count, out_count = lax.axis_size("hid"), lax.axis_size("out")
    out_index, rep_index = lax.axis_index("out"), lax.axis_index("rep")
    token_count, width = x_act.shape[1:]
    mine = token_count // out_count
    few = mine // hid_count
    code_rows = weight_codes.shape[0]
    grads_out = out_grad[0]
    signs = sign_rows(hid_count, few)
    root = math.sqrt(hid_count)

    tokens = lax.dynamic_slice_in_dim(x_act[0], out_index * mine, mine, axis=0)
    rows = trade(tokens.reshape(hid_count, few, width), "hid").reshape(mine, width)

    scales = jnp.exp2(group_exps.astype(jnp.float32)).astype(jnp.bfloat16)
    lanes = np.repeat(np.eye(width // GROUP, dtype=np.float32), GROUP, axis=1)
    scales = jnp.dot(scales, lanes.astype(jnp.bfloat16), preferred_element_type=jnp.float32)
    w_deq = (weight_codes.astype(jnp.float32) * scales).astype(jnp.bfloat16)
    w_other = partner(w_deq, "rep", 1)
    factor = gather_factor(local_factor)

    grads_t = grads_out.T
    g_own = lax.dynamic_slice_in_dim(grads_out, rep_index * code_rows, code_rows, axis=1)
    g_other = lax.dynamic_slice_in_dim(grads_out, (1 - rep_index) * code_rows, code_rows, axis=1)
    gt_own = lax.dynamic_slice_in_dim(grads_t, rep_index * code_rows, code_rows, axis=0)
    gt_other = lax.dynamic_slice_in_dim(grads_t, (1 - rep_index) * code_rows, code_rows, axis=0)
    g_own, g_other, gt_own, gt_other = lax.optimization_barrier((g_own, g_other, gt_own, gt_other))
    partial_rot = jnp.dot(g_own, w_deq, preferred_element_type=jnp.float32) + jnp.dot(
        g_other, w_other, preferred_element_type=jnp.float32
    )
    partial_rot = partial_rot.astype(jnp.bfloat16).reshape(out_count, mine, width)
    pieces = trade(partial_rot, "out")

    grad_rot = pieces.astype(jnp.float32).sum(axis=0).astype(jnp.bfloat16)
    grad_mix = mix_blocks(grad_rot)

    mixed = jnp.dot(signs.astype(jnp.bfloat16), rows, preferred_element_type=jnp.float32)
    mixed = (mixed / root).astype(jnp.bfloat16).reshape(hid_count, few, width)
    mixed = trade(mixed, "hid").reshape(mine, width)
    mixed = jnp.broadcast_to(mixed[None], (out_count, mine, width))
    mixed = trade(mixed, "out").reshape(token_count, width)

    high = lax.reduce_precision(grad_mix, exponent_bits=8, mantissa_bits=7)
    low = (grad_mix - high).astype(jnp.bfloat16)
    across = (((1,), (1,)), ((), ()))
    back = lax.dot_general(
        high.astype(jnp.bfloat16), factor, across, preferred_element_type=jnp.float32
    ) + lax.dot_general(low, factor, across, preferred_element_type=jnp.float32)
    input_grad = back.astype(jnp.bfloat16)[None]

    away = jnp.dot(gt_other, mixed, preferred_element_type=jnp.float32)
    away = away.astype(jnp.bfloat16)
    arrived = partner(away, "rep", 1)
    own = jnp.dot(gt_own, mixed, preferred_element_type=jnp.float32)
    own = lax.optimization_barrier(own)
    weight_grad = (own + arrived.astype(jnp.float32)).astype(jnp.bfloat16)
    weight_grad = jnp.dot(weight_grad, factor, preferred_element_type=jnp.float32)
    return (input_grad,) + adam(weight_grad, weight_codes, first_moment, second_moment)


def adam(weight_grad, weight_codes, first_moment, second_moment):
    gradient = jnp.where(jnp.abs(weight_codes) <= 126, weight_grad / 16.0, jnp.float32(0.0))
    moment_one = 0.9 * first_moment.astype(jnp.float32) + 0.1 * gradient
    moment_two = 0.95 * second_moment.astype(jnp.float32) + 0.05 * gradient * gradient
    corr_one = 1.0 - 0.9**20
    corr_two = 1.0 - 0.95**20
    weight_step = moment_one / corr_one / (jnp.sqrt(moment_two / corr_two) + 1e-08)
    return (
        weight_step.astype(jnp.bfloat16),
        moment_one.astype(jnp.bfloat16),
        moment_two.astype(jnp.bfloat16),
    )


def solution(mesh):
    placed = (
        P("rep", None, "hid"),
        P("rep", None, "out"),
        P(("out", "rep"), "hid"),
        P(("out", "rep"), "hid"),
        P(("out", "rep"), None),
        P(("out", "rep"), "hid"),
        P(("out", "rep"), "hid"),
    )
    return jax.shard_map(
        step,
        mesh=mesh,
        in_specs=placed,
        out_specs=(
            P("rep", "out", "hid"),
            P(("out", "rep"), "hid"),
            P(("out", "rep"), "hid"),
            P(("out", "rep"), "hid"),
        ),
        check_vma=False,
    )
```

```python
import math

import jax
import jax.numpy as jnp
import numpy as np
from jax import lax
from jax.experimental import pallas as pl
from jax.experimental.pallas import tpu as pltpu
from jax.sharding import PartitionSpec as P


GROUP = 128


def trade(block, axis):
    return lax.all_to_all(block, axis, split_axis=0, concat_axis=0, tiled=True)


def partner(block, axis, bit):
    count = lax.axis_size(axis)
    return lax.ppermute(block, axis, [(s, s ^ bit) for s in range(count)])


KERNEL_VMEM = pltpu.CompilerParams(vmem_limit_bytes=8 * 1024 * 1024)


def dequant_kernel(codes, exps, factor, out):
    rows = codes.shape[0]
    scales = jnp.exp2(exps[...].astype(jnp.float32))
    for group in range(exps.shape[1]):
        lanes = slice(group * GROUP, (group + 1) * GROUP)
        values = codes[:, lanes].astype(jnp.float32) * scales[:, group : group + 1]
        out[0:rows, lanes] = values.astype(out.dtype)
    out[rows:, :] = factor[...]


def dequantize(codes, exps, factor):
    rows, width = codes.shape
    whole = pl.BlockSpec(memory_space=pltpu.VMEM)
    return pl.pallas_call(
        dequant_kernel,
        out_shape=jax.ShapeDtypeStruct((rows + factor.shape[0], width), factor.dtype),
        in_specs=[whole] * 3,
        out_specs=whole,
        compiler_params=KERNEL_VMEM,
        cost_estimate=pl.CostEstimate(
            flops=2 * rows * width, bytes_accessed=6 * rows * width, transcendentals=0
        ),
    )(codes, exps, factor)


def order_kernel(place, mine, other, out):
    spot, core = place[0], place[1]
    for index in range(mine.shape[0]):
        source = index ^ spot

        @pl.when(core == 0)
        def _():
            out[index, 0] = mine[source]
            out[index, 1] = other[source]

        @pl.when(core == 1)
        def _():
            out[index, 0] = other[source]
            out[index, 1] = mine[source]


def in_order(mine, other, spot, core):
    count, rows, width = mine.shape
    whole = pl.BlockSpec(memory_space=pltpu.VMEM)
    return pl.pallas_call(
        order_kernel,
        out_shape=jax.ShapeDtypeStruct((count, 2, rows, width), mine.dtype),
        in_specs=[pl.BlockSpec(memory_space=pltpu.SMEM), whole, whole],
        out_specs=whole,
        compiler_params=KERNEL_VMEM,
        cost_estimate=pl.CostEstimate(
            flops=0, bytes_accessed=8 * count * rows * width, transcendentals=0
        ),
    )(jnp.stack([spot, core]), mine, other)


def sign_rows(count, inner):
    index = np.arange(count * inner)
    upper, lower = index // inner, index % inner
    both = upper[:, None] & upper[None, :]
    parity = np.zeros_like(both)
    for bit in range(count.bit_length()):
        parity ^= both >> bit & 1
    same = lower[:, None] == lower[None, :]
    return ((1 - 2 * parity) * same).astype(np.float32)


def gather_factor(local_factor, other):
    core, spot = lax.axis_index("hid") % 2, lax.axis_index("out")
    _, width = local_factor.shape
    bits = lax.axis_size("out").bit_length() - 1
    block = jnp.where(core == lax.axis_index("rep"), local_factor, other)[None]
    for bit in range(bits):
        other = partner(block, "out", 1 << bit)
        block = jnp.concatenate([block, other], axis=0)
    other = partner(block, "hid", 1)
    return in_order(block, other, spot, core).reshape(width, width)


def mix_blocks(block):
    where = lax.axis_index("hid")
    count = lax.axis_size("hid")
    total = block
    for bit in reversed(range(count.bit_length() - 1)):
        sent = total if bit < 2 else total.astype(jnp.bfloat16)
        other = partner(sent, "hid", 1 << bit).astype(jnp.float32)
        sign = 1.0 - 2.0 * (where >> bit & 1).astype(jnp.float32)
        total = other + sign * total.astype(jnp.float32)
    return total / math.sqrt(count)


def step(x_act, out_grad, weight_codes, group_exps, local_factor, first_moment, second_moment):
    hid_count, out_count = lax.axis_size("hid"), lax.axis_size("out")
    out_index, rep_index = lax.axis_index("out"), lax.axis_index("rep")
    token_count, width = x_act.shape[1:]
    mine = token_count // out_count
    few = mine // hid_count
    code_rows = weight_codes.shape[0]
    grads_out = out_grad[0]
    signs = sign_rows(hid_count, few)
    root = math.sqrt(hid_count)

    tokens = lax.dynamic_slice_in_dim(x_act[0], out_index * mine, mine, axis=0)
    rows = trade(tokens.reshape(hid_count, few, width), "hid").reshape(mine, width)

    sent = dequantize(weight_codes, group_exps, local_factor)
    arrived = partner(sent, "rep", 1)
    w_deq, w_other = sent[:code_rows], arrived[:code_rows]
    factor = gather_factor(local_factor, arrived[code_rows:])

    grads_t = grads_out.T
    g_own = lax.dynamic_slice_in_dim(grads_out, rep_index * code_rows, code_rows, axis=1)
    g_other = lax.dynamic_slice_in_dim(grads_out, (1 - rep_index) * code_rows, code_rows, axis=1)
    gt_own = lax.dynamic_slice_in_dim(grads_t, rep_index * code_rows, code_rows, axis=0)
    gt_other = lax.dynamic_slice_in_dim(grads_t, (1 - rep_index) * code_rows, code_rows, axis=0)
    g_own, g_other, gt_own, gt_other = lax.optimization_barrier((g_own, g_other, gt_own, gt_other))
    partial_rot = jnp.dot(g_own, w_deq, preferred_element_type=jnp.float32) + jnp.dot(
        g_other, w_other, preferred_element_type=jnp.float32
    )
    partial_rot = partial_rot.astype(jnp.bfloat16).reshape(out_count, mine, width)
    pieces = trade(partial_rot, "out")

    grad_rot = pieces.astype(jnp.float32).sum(axis=0).astype(jnp.bfloat16)
    grad_mix = mix_blocks(grad_rot)

    mixed = jnp.dot(signs.astype(jnp.bfloat16), rows, preferred_element_type=jnp.float32)
    mixed = (mixed / root).astype(jnp.bfloat16).reshape(hid_count, few, width)
    mixed = trade(mixed, "hid").reshape(mine, width)
    mixed = jnp.broadcast_to(mixed[None], (out_count, mine, width))
    mixed = trade(mixed, "out").reshape(token_count, width)

    high = lax.reduce_precision(grad_mix, exponent_bits=8, mantissa_bits=7)
    low = (grad_mix - high).astype(jnp.bfloat16)
    across = (((1,), (1,)), ((), ()))
    back = lax.dot_general(
        high.astype(jnp.bfloat16), factor, across, preferred_element_type=jnp.float32
    ) + lax.dot_general(low, factor, across, preferred_element_type=jnp.float32)
    input_grad = back.astype(jnp.bfloat16)[None]

    away = jnp.dot(gt_other, mixed, preferred_element_type=jnp.float32)
    away = away.astype(jnp.bfloat16)
    arrived = partner(away, "rep", 1)
    own = jnp.dot(gt_own, mixed, preferred_element_type=jnp.float32)
    own = lax.optimization_barrier(own)
    weight_grad = (own + arrived.astype(jnp.float32)).astype(jnp.bfloat16)
    weight_grad = jnp.dot(weight_grad, factor, preferred_element_type=jnp.float32)
    return (input_grad,) + adam(weight_grad, weight_codes, first_moment, second_moment)


def adam(weight_grad, weight_codes, first_moment, second_moment):
    gradient = jnp.where(jnp.abs(weight_codes) <= 126, weight_grad / 16.0, jnp.float32(0.0))
    moment_one = 0.9 * first_moment.astype(jnp.float32) + 0.1 * gradient
    moment_two = 0.95 * second_moment.astype(jnp.float32) + 0.05 * gradient * gradient
    corr_one = 1.0 - 0.9**20
    corr_two = 1.0 - 0.95**20
    weight_step = moment_one / corr_one / (jnp.sqrt(moment_two / corr_two) + 1e-08)
    return (
        weight_step.astype(jnp.bfloat16),
        moment_one.astype(jnp.bfloat16),
        moment_two.astype(jnp.bfloat16),
    )


def solution(mesh):
    placed = (
        P("rep", None, "hid"),
        P("rep", None, "out"),
        P(("out", "rep"), "hid"),
        P(("out", "rep"), "hid"),
        P(("out", "rep"), None),
        P(("out", "rep"), "hid"),
        P(("out", "rep"), "hid"),
    )
    return jax.shard_map(
        step,
        mesh=mesh,
        in_specs=placed,
        out_specs=(
            P("rep", "out", "hid"),
            P(("out", "rep"), "hid"),
            P(("out", "rep"), "hid"),
            P(("out", "rep"), "hid"),
        ),
        check_vma=False,
    )
```

```python
import math

import jax
import jax.numpy as jnp
import numpy as np
from jax import lax
from jax.experimental import pallas as pl
from jax.experimental.pallas import tpu as pltpu
from jax.sharding import PartitionSpec as P


GROUP = 128


def trade(block, axis, order=None):
    groups = None if order is None else [order]
    return lax.all_to_all(
        block, axis, split_axis=0, concat_axis=0, tiled=True, axis_index_groups=groups
    )


def partner(block, axis, bit):
    count = lax.axis_size(axis)
    return lax.ppermute(block, axis, [(s, s ^ bit) for s in range(count)])


KERNEL_VMEM = pltpu.CompilerParams(vmem_limit_bytes=8 * 1024 * 1024)


def order_kernel(place, mine, other, out):
    spot, core = place[0], place[1]
    for index in range(mine.shape[0]):
        source = index ^ spot

        @pl.when(core == 0)
        def _():
            out[index, 0] = mine[source]
            out[index, 1] = other[source]

        @pl.when(core == 1)
        def _():
            out[index, 0] = other[source]
            out[index, 1] = mine[source]


def in_order(mine, other, spot, core):
    count, rows, width = mine.shape
    whole = pl.BlockSpec(memory_space=pltpu.VMEM)
    return pl.pallas_call(
        order_kernel,
        out_shape=jax.ShapeDtypeStruct((count, 2, rows, width), mine.dtype),
        in_specs=[pl.BlockSpec(memory_space=pltpu.SMEM), whole, whole],
        out_specs=whole,
        compiler_params=KERNEL_VMEM,
        cost_estimate=pl.CostEstimate(
            flops=0, bytes_accessed=8 * count * rows * width, transcendentals=0
        ),
    )(jnp.stack([spot, core]), mine, other)


def sign_rows(order, inner):
    upper = np.repeat(np.array(order), inner)
    lower = np.arange(upper.size) % inner
    both = upper[:, None] & upper[None, :]
    parity = np.zeros_like(both)
    for bit in range(len(order).bit_length()):
        parity ^= both >> bit & 1
    same = lower[:, None] == lower[None, :]
    return ((1 - 2 * parity) * same).astype(np.float32)


def gather_factor(local_factor, other):
    core, spot = lax.axis_index("hid") % 2, lax.axis_index("out")
    _, width = local_factor.shape
    bits = lax.axis_size("out").bit_length() - 1
    block = jnp.where(core == lax.axis_index("rep"), local_factor, other)[None]
    for bit in range(bits):
        other = partner(block, "out", 1 << bit)
        block = jnp.concatenate([block, other], axis=0)
    other = partner(block, "hid", 1)
    return in_order(block, other, spot, core).reshape(width, width)


def mix_blocks(block):
    where = lax.axis_index("hid")
    count = lax.axis_size("hid")
    total = block
    bits = count.bit_length() - 1
    turns = [*range(bits - 2, 1, -1), bits - 1, *range(min(bits - 1, 2) - 1, -1, -1)]
    for bit in turns:
        sent = total if bit < 2 else total.astype(jnp.bfloat16)
        other = partner(sent, "hid", 1 << bit).astype(jnp.float32)
        sign = 1.0 - 2.0 * (where >> bit & 1).astype(jnp.float32)
        total = other + sign * total.astype(jnp.float32)
    return total / math.sqrt(count)


def step(x_act, out_grad, weight_codes, group_exps, local_factor, first_moment, second_moment):
    hid_count, out_count = lax.axis_size("hid"), lax.axis_size("out")
    out_index, rep_index = lax.axis_index("out"), lax.axis_index("rep")
    token_count, width = x_act.shape[1:]
    mine = token_count // out_count
    few = mine // hid_count
    code_rows = weight_codes.shape[0]
    grads_out = out_grad[0]
    order = [index ^ hid_count // 2 for index in range(hid_count)]
    signs = sign_rows(order, few)
    root = math.sqrt(hid_count)

    tokens = lax.dynamic_slice_in_dim(x_act[0], out_index * mine, mine, axis=0)
    rows = trade(tokens.reshape(hid_count, few, width), "hid", order).reshape(mine, width)

    scales = jnp.exp2(group_exps.astype(jnp.float32)).astype(jnp.bfloat16)
    lanes = np.repeat(np.eye(width // GROUP, dtype=np.float32), GROUP, axis=1)
    scales = jnp.dot(scales, lanes.astype(jnp.bfloat16), preferred_element_type=jnp.float32)
    w_deq = (weight_codes.astype(jnp.float32) * scales).astype(jnp.bfloat16)
    sent = jnp.concatenate([w_deq, local_factor], axis=0)
    arrived = partner(sent, "rep", 1)
    w_other = arrived[:code_rows]
    factor = gather_factor(local_factor, arrived[code_rows:])

    grads_t = grads_out.T
    g_own = lax.dynamic_slice_in_dim(grads_out, rep_index * code_rows, code_rows, axis=1)
    g_other = lax.dynamic_slice_in_dim(grads_out, (1 - rep_index) * code_rows, code_rows, axis=1)
    gt_own = lax.dynamic_slice_in_dim(grads_t, rep_index * code_rows, code_rows, axis=0)
    gt_other = lax.dynamic_slice_in_dim(grads_t, (1 - rep_index) * code_rows, code_rows, axis=0)
    g_own, g_other, gt_own, gt_other = lax.optimization_barrier((g_own, g_other, gt_own, gt_other))
    partial_rot = jnp.dot(g_own, w_deq, preferred_element_type=jnp.float32) + jnp.dot(
        g_other, w_other, preferred_element_type=jnp.float32
    )
    partial_rot = partial_rot.astype(jnp.bfloat16).reshape(out_count, mine, width)
    pieces = trade(partial_rot, "out")

    grad_rot = pieces.astype(jnp.float32).sum(axis=0).astype(jnp.bfloat16)
    grad_mix = mix_blocks(grad_rot)

    mixed = jnp.dot(signs.astype(jnp.bfloat16), rows, preferred_element_type=jnp.float32)
    mixed = (mixed / root).astype(jnp.bfloat16).reshape(hid_count, few, width)
    mixed = trade(mixed, "hid", order).reshape(mine, width)
    mixed = jnp.broadcast_to(mixed[None], (out_count, mine, width))
    mixed = trade(mixed, "out").reshape(token_count, width)

    high = lax.reduce_precision(grad_mix, exponent_bits=8, mantissa_bits=7)
    low = (grad_mix - high).astype(jnp.bfloat16)
    across = (((1,), (1,)), ((), ()))
    back = lax.dot_general(
        high.astype(jnp.bfloat16), factor, across, preferred_element_type=jnp.float32
    ) + lax.dot_general(low, factor, across, preferred_element_type=jnp.float32)
    input_grad = back.astype(jnp.bfloat16)[None]

    away = jnp.dot(gt_other, mixed, preferred_element_type=jnp.float32)
    away = away.astype(jnp.bfloat16)
    arrived = partner(away, "rep", 1)
    own = jnp.dot(gt_own, mixed, preferred_element_type=jnp.float32)
    own = lax.optimization_barrier(own)
    weight_grad = (own + arrived.astype(jnp.float32)).astype(jnp.bfloat16)
    weight_grad = jnp.dot(weight_grad, factor, preferred_element_type=jnp.float32)
    return (input_grad,) + adam(weight_grad, weight_codes, first_moment, second_moment)


def adam(weight_grad, weight_codes, first_moment, second_moment):
    gradient = jnp.where(jnp.abs(weight_codes) <= 126, weight_grad / 16.0, jnp.float32(0.0))
    moment_one = 0.9 * first_moment.astype(jnp.float32) + 0.1 * gradient
    moment_two = 0.95 * second_moment.astype(jnp.float32) + 0.05 * gradient * gradient
    corr_one = 1.0 - 0.9**20
    corr_two = 1.0 - 0.95**20
    weight_step = moment_one / corr_one / (jnp.sqrt(moment_two / corr_two) + 1e-08)
    return (
        weight_step.astype(jnp.bfloat16),
        moment_one.astype(jnp.bfloat16),
        moment_two.astype(jnp.bfloat16),
    )


def solution(mesh):
    placed = (
        P("rep", None, "hid"),
        P("rep", None, "out"),
        P(("out", "rep"), "hid"),
        P(("out", "rep"), "hid"),
        P(("out", "rep"), None),
        P(("out", "rep"), "hid"),
        P(("out", "rep"), "hid"),
    )
    return jax.shard_map(
        step,
        mesh=mesh,
        in_specs=placed,
        out_specs=(
            P("rep", "out", "hid"),
            P(("out", "rep"), "hid"),
            P(("out", "rep"), "hid"),
            P(("out", "rep"), "hid"),
        ),
        check_vma=False,
    )
```
